256 devices in a mesh: pipe: 16 (over z, core), expert: 16 (over x, y).
Axes of the slice: x: 4, y: 4, z: 8, core: 2. Of those that a mesh axis runs over, the one named last changes fastest.
Arguments:
- section_inputs: bfloat16 [16, 4, 512, 4096], P('pipe', None, 'expert'), may hold values from -6 to 6
- out_grad: bfloat16 [16, 4, 512, 4096], P('pipe', None, 'expert'), may hold values from -6 to 6
- norm_gain: float32 [8, 4096], replicated, may hold values from 0.5 to 1.5
- route_ids: int32 [16, 4, 512, 1], P('pipe', None, 'expert'), may hold values from 0 to 15; in each aligned block of 32 rows (0 to 31, 32 to 63, ..., all dimensions but the last counted through in order) at most 3 rows name the same one
- route_weight: float32 [16, 4, 512, 1], P('pipe', None, 'expert'), may hold values from 0.2 to 1
- w_gate: bfloat16 [16, 16, 4096, 384], P('pipe', 'expert'), may hold values from -0.09375 to 0.09375
- w_up: bfloat16 [16, 16, 4096, 384], P('pipe', 'expert'), may hold values from -0.09375 to 0.09375
- w_down: bfloat16 [16, 16, 384, 4096], P('pipe', 'expert'), may hold values from -0.21875 to 0.21875
Outputs:
- input_grad: bfloat16 [16, 4, 512, 4096], P('pipe', None, 'expert')
The draws below stay inside these ranges and needn't reach their ends.
Inputs may be any that keep to these rules, and one draw needn't show every extreme that they name: `route_ids`: each token has exactly one route, naming one expert. In each micro-batch and lane, every aligned block of 32 tokens (the tokens of one device) names one expert at most 3 times, a bound that some block reaches.
All inputs are finite; a program needn't handle non-finite values.
Results may differ from the reference program's by a relative error of at most 0.025.
Values may be sent and summed in bfloat16 or wider, within the bound.
A program may use at most 128 MiB of HBM per device.

```python
import math
import jax
import jax.numpy as jnp
import numpy as np
from jax import lax

D = 4096
FF = 768
FH = 384
T_MB = 32
MB = 4
TOP = 1
SECTIONS = 8
EXPERTS = 16
TOK_E = 512
CAP = 3
N_PIPE = 16
N_EXPERT = 16


def levels(key, dims, shards, low, largest):
    level, own = 1.0, jax.random.fold_in(key, 6)
    for dim, blocks in shards:
        draws = jnp.exp(jax.random.uniform(jax.random.fold_in(own, dim), (blocks,), jnp.float32, low / len(shards), largest / len(shards)))
        level = level * jnp.repeat(draws, dims[dim] // blocks).reshape([-1 if axis == dim else 1 for axis in range(len(dims))])
    return level


def deal_out(rng, own, number, rows, number_of, top, limit, skew):
    ranking = jax.random.permutation(rng, number_of)
    heavy_load, ordinary = portions_of(number_of, rows * top, limit, skew, True), portions_of(number_of, rows * top, limit, skew, False)
    places = jnp.arange(number_of)

    def named(tallies, offset_by):
        used = int((tallies > 0).sum())
        fixed = max(1, used // 4)
        passed = fixed + (places - fixed + offset_by * (used - fixed)) % max(1, number_of - fixed)
        return jnp.zeros((number_of,), jnp.int32).at[ranking[jnp.where(places < fixed, places, passed)]].set(jnp.asarray(tallies, jnp.int32))

    tallies = jnp.where(number % 4 == 0, named(heavy_load, number // 4), named(ordinary, number - number // 4 - 1))
    mixed = jax.random.permutation(jax.random.fold_in(own, 3), number_of)
    source_of, sink = mixed[0:number_of // 2 * 2:2], mixed[1:number_of // 2 * 2:2]
    slack = jnp.minimum(tallies[source_of] - 1, limit - tallies[sink]) // 2
    slack = jnp.where((source_of == ranking[0]) | (sink == ranking[0]) | (tallies[sink] == 0), 0, jnp.maximum(slack, 0))
    passed = jax.random.randint(jax.random.fold_in(own, 4), (number_of // 2,), 0, 1 << 20) % (slack + 1)
    tallies = tallies.at[source_of].add(-passed).at[sink].add(passed)
    items = jnp.searchsorted(jnp.cumsum(tallies), jnp.arange(rows * top), side="right").astype(jnp.int32)
    table = items.reshape(top, rows).T
    table = table[jax.random.permutation(jax.random.fold_in(own, 1), rows)]
    offset_by = jax.random.randint(jax.random.fold_in(own, 2), (rows, 1), 0, top)
    return jnp.take_along_axis(table, (jnp.arange(top)[None, :] + offset_by) % top, axis=1)


def portions_of(number_of, total, reach, slope, full):
    portions = [(1 << 20) // math.isqrt(rank ** slope) + 1 for rank in range(1, number_of + 1)]
    largest = reach if full else min(reach, max(-(-total // number_of), total * portions[0] // sum(portions)))
    least = 1 if total - largest >= number_of - 1 else 0
    holding, rest = [largest] + [least] * (number_of - 1), total - largest - least * (number_of - 1)
    while rest > 0:
        movable = [i for i in range(1, number_of) if holding[i] < largest] or [i for i in range(1, number_of) if holding[i] < reach]
        whole, left = sum([portions[i] for i in movable]), rest
        for i in movable:
            extra = min(reach - holding[i], max(1, left * portions[i] // whole), rest)
            holding[i] = holding[i] + extra
            rest = rest - extra
    return np.array(holding)


def noise(own_key, dims, spread, most, cuts=(), held_as=jnp.bfloat16):
    gain = levels(own_key, dims, cuts, -0.22, 0.18) if cuts else 1.0
    values = jax.random.normal(own_key, dims, jnp.float32) * spread * gain
    return jnp.minimum(jnp.maximum(values, -most), most).astype(held_as)


def setup_inputs(seed: int = 0) -> dict:
    key_of = jax.random.split(jax.random.key(seed), 9)
    section_inputs = noise(key_of[0], (N_PIPE, MB, TOK_E, D), 1.0, 6.0, ((0, 16), (2, 16)))
    out_grad = noise(key_of[1], (N_PIPE, MB, TOK_E, D), 1.0, 6.0, ((0, 16), (2, 16)))
    norm_gain = jnp.clip(1.0 + 0.1 * jax.random.normal(key_of[2], (SECTIONS, D), jnp.float32), 0.5, 1.5)
    route_ids_keys = jax.random.split(jax.random.fold_in(key_of[3], 1), N_PIPE * MB * TOK_E // T_MB)
    route_ids_turns = jax.random.permutation(jax.random.fold_in(key_of[3], 3), N_PIPE * MB * TOK_E // T_MB)
    route_ids = jax.vmap(lambda own, number: deal_out(jax.random.fold_in(key_of[3], 2), own, number, T_MB, EXPERTS, TOP, CAP, 2))(route_ids_keys, route_ids_turns).reshape((N_PIPE, MB, TOK_E, TOP))
    route_weight = jnp.clip(jnp.exp(math.log(1.0) - 1.609438 * jax.random.uniform(key_of[4], (N_PIPE, MB, TOK_E, TOP), jnp.float32) ** levels(key_of[4], (N_PIPE, MB, TOK_E, TOP), ((0, 16), (2, 16)), -0.2, 0.2)), 0.2, 1.0)
    w_gate = noise(key_of[5], (N_PIPE, EXPERTS, D, FH), D ** -0.5, 0.09375, ((0, 16), (1, 16)))
    w_up = noise(key_of[6], (N_PIPE, EXPERTS, D, FH), D ** -0.5, 0.09375, ((0, 16), (1, 16)))
    w_down = noise(key_of[7], (N_PIPE, EXPERTS, FH, D), FF ** -0.5, 0.21875, ((0, 16), (1, 16)))
    return dict(section_inputs=section_inputs, out_grad=out_grad, norm_gain=norm_gain, route_ids=route_ids, route_weight=route_weight, w_gate=w_gate, w_up=w_up, w_down=w_down)


EPS = 1e-06

def expert_grad(x_rows, d_rows, wg, wu, wd):
    gate = jnp.dot(x_rows, wg, preferred_element_type=jnp.float32)
    up = jnp.dot(x_rows, wu, preferred_element_type=jnp.float32)
    grad_act = jnp.dot(d_rows, wd.T, preferred_element_type=jnp.float32)
    sig = jax.nn.sigmoid(gate)
    dgate = (grad_act * up * sig * (1.0 + gate * (1.0 - sig))).astype(jnp.bfloat16)
    dup = (grad_act * gate * sig).astype(jnp.bfloat16)
    total = jnp.dot(dgate, wg.T, preferred_element_type=jnp.float32) + jnp.dot(dup, wu.T, preferred_element_type=jnp.float32)
    return total.astype(jnp.bfloat16)

def section_grad(x, output_gradient, norm_weight, ids, weights, wg_pair, wu_pair, wd_pair):
    input_float = x.astype(jnp.float32)
    inverse_norm_scale = lax.rsqrt(lax.optimization_barrier(jnp.mean(input_float * input_float, axis=-1, keepdims=True)) + EPS)
    unit_input = input_float * inverse_norm_scale
    normed_input = (unit_input * norm_weight).astype(jnp.bfloat16)
    flat = ids.reshape(-1)
    rows_e = 2 * N_EXPERT * CAP

    def per_expert(expert):
        order = jnp.argsort((flat != expert).astype(jnp.int32), stable=True)[:rows_e].astype(jnp.int32)
        valid = flat[order] == expert
        tokens = order // TOP
        x_rows = normed_input[tokens]
        d_rows = jnp.where(valid[:, None], output_gradient[tokens], jnp.zeros_like(output_gradient[tokens]))
        first = expert_grad(x_rows, d_rows, wg_pair[0, expert], wu_pair[0, expert], wd_pair[0, expert])
        second = expert_grad(x_rows, d_rows, wg_pair[1, expert], wu_pair[1, expert], wd_pair[1, expert])
        both = (first.astype(jnp.float32) + second.astype(jnp.float32)).astype(jnp.bfloat16)
        return (order, valid, both)
    orders, valids, contrib = lax.map(per_expert, jnp.arange(EXPERTS, dtype=jnp.int32))
    masked = jnp.where(valids[..., None], contrib.astype(jnp.float32), jnp.float32(0.0))
    routes = jnp.zeros((flat.shape[0], x.shape[1]), jnp.float32).at[orders.reshape(-1)].add(masked.reshape(-1, x.shape[1]))
    routes = routes.reshape(x.shape[0], TOP, x.shape[1])
    dxn = lax.optimization_barrier(jnp.sum(routes * weights[:, :, None], axis=1))
    weighted_gradient = dxn * norm_weight
    section_output = output_gradient.astype(jnp.float32) + inverse_norm_scale * (weighted_gradient - unit_input * lax.optimization_barrier(jnp.mean(weighted_gradient * unit_input, axis=-1, keepdims=True)))
    return section_output.astype(jnp.bfloat16)

def lanes_join(arr):
    joined = jnp.swapaxes(arr, 0, 1)
    return joined.reshape((joined.shape[0], joined.shape[1] * joined.shape[2]) + joined.shape[3:])

def reference(section_inputs, out_grad, norm_gain, route_ids, route_weight, w_gate, w_up, w_down):
    grads = []
    above = None
    for section in reversed(range(SECTIONS)):
        low = 2 * section
        x = lanes_join(section_inputs[low:low + 2])
        if section == SECTIONS - 1:
            output_gradient = lanes_join(out_grad[low:low + 2])
        else:
            output_gradient = above
        ids = lanes_join(route_ids[low:low + 2])
        weights = lanes_join(route_weight[low:low + 2])
        norm_weight = norm_gain[section]
        wg_pair = w_gate[low:low + 2]
        wu_pair = w_up[low:low + 2]
        wd_pair = w_down[low:low + 2]

        def one(operands):
            return section_grad(operands[0], operands[1], norm_weight, operands[2], operands[3], wg_pair, wu_pair, wd_pair)
        section_output = lax.map(one, (x, output_gradient, ids, weights))
        above = section_output
        grads.append(jnp.swapaxes(section_output.reshape(MB, 2, TOK_E, D), 0, 1))
    return jnp.concatenate(grads[::-1], axis=0)
```

```python
import jax
import jax.numpy as jnp
from jax import lax
from jax.experimental import pallas as pl
from jax.experimental.pallas import tpu as pltpu
from jax.sharding import PartitionSpec as P

EPS = 1e-06
MESH = pl.DeviceIdType.MESH
BF = jnp.bfloat16
F32 = jnp.float32
CAP = 3
NC = 2


def dot_t(a, b):
    return lax.dot_general(a, b, (((1,), (1,)), ((), ())), preferred_element_type=F32)


def make_kernel(MB, T, D, FH, LANES, PEERS):
    SEC = LANES // 2
    SLOTS = PEERS * CAP
    SUB = D // 128
    CS = SUB // NC
    CD = D // NC
    FF = 2 * FH

    def kernel(tok_ref, cidx_ref, slotup_ref, x_hbm, og_hbm, wtab_hbm, gain_ref, wg_hbm, wu_hbm, wd_hbm, out_hbm,
               xv, ov, xrow, orow, sendx, recvx, sendd, recvd, sendr, xstd, xn, dys, ostd, fa, fb, fc, rs, wtab, wrecv, wrow,
               wg, wu, wd, fin, outstd,
               ret00, ret01, ret10, ret11, ret20, ret21, ret30, ret31,
               in_sem, wl_sem, wrs_sem, wrr_sem, ts_sem, tr_sem, xs_sem, xr_sem, ds_sem, dr_sem, rsnd_sem, rr_sem,
               os_sem, or_sem):
        rets = ((ret00, ret01), (ret10, ret11), (ret20, ret21), (ret30, ret31))
        p = lax.axis_index("pipe")
        e = lax.axis_index("expert")
        s = p // 2
        h = p % 2
        down = (p + LANES - 2) % LANES
        up = (p + 2) % LANES
        mate = p + 1 - 2 * h
        top = s == SEC - 1

        def local_in(src, dst, i):
            return pltpu.make_async_copy(src, dst, in_sem.at[i])

        in_x = local_in(x_hbm, xv, 0)
        in_o = local_in(og_hbm, ov, 1)
        in_t = local_in(wtab_hbm, wtab, 2)
        in_x.start()
        in_t.start()
        in_o.start()
        gcol = pl.ds(pl.multiple_of(h * FH, 128), FH)
        drow = pl.ds(pl.multiple_of(h * FH, 128), FH)
        lw = (
            pltpu.make_async_copy(wg_hbm, wg.at[:, gcol], wl_sem.at[0]),
            pltpu.make_async_copy(wu_hbm, wu.at[:, gcol], wl_sem.at[1]),
            pltpu.make_async_copy(wd_hbm, wd.at[drow, :], wl_sem.at[2]),
        )
        for c in lw:
            c.start()

        barrier = pltpu.get_barrier_semaphore()

        def sig_plane(k, _):
            pl.semaphore_signal(barrier, inc=1, device_id=(p, (e + k) % PEERS), device_id_type=MESH)
            return 0

        lax.fori_loop(1, PEERS, sig_plane, 0)

        def sig_z(k, _):
            peer = (e + k) % PEERS
            pl.semaphore_signal(barrier, inc=1, device_id=(down, peer), device_id_type=MESH)
            pl.semaphore_signal(barrier, inc=1, device_id=(up, peer), device_id_type=MESH)
            return 0

        lax.fori_loop(0, PEERS, sig_z, 0)
        pl.semaphore_signal(barrier, inc=1, device_id=(mate, e), device_id_type=MESH)
        pl.semaphore_wait(barrier, PEERS - 1 + 2 * PEERS + 1)

        def rcopy(src, dst, ssem, rsem, dev):
            return pltpu.make_async_remote_copy(
                src_ref=src, dst_ref=dst, send_sem=ssem, recv_sem=rsem, device_id=dev, device_id_type=MESH
            )

        rw = (
            rcopy(wg_hbm, wg.at[:, gcol], wrs_sem.at[0], wrr_sem.at[0], (mate, e)),
            rcopy(wu_hbm, wu.at[:, gcol], wrs_sem.at[1], wrr_sem.at[1], (mate, e)),
            rcopy(wd_hbm, wd.at[drow, :], wrs_sem.at[2], wrr_sem.at[2], (mate, e)),
        )
        for c in rw:
            c.start()

        mine = pl.ds(e * CAP, CAP)

        def send_x(m):
            for k in range(SLOTS):
                sendx[m, k] = xrow[m * T + tok_ref[m * SLOTS + k]]
            recvx[m, mine] = sendx[m, mine]

            def go(k, _):
                peer = (e + k) % PEERS
                rcopy(sendx.at[m, pl.ds(peer * CAP, CAP)], recvx.at[m, mine], xs_sem.at[m], xr_sem.at[m], (p, peer)).start()
                return 0

            lax.fori_loop(1, PEERS, go, 0)

        def wait_x(m):
            return rcopy(
                sendx.at[m, pl.ds(0, SLOTS - CAP)], recvx.at[m, pl.ds(0, SLOTS - CAP)], xs_sem.at[m], xr_sem.at[m], (p, e)
            )

        def send_d(m, c):
            recvd[m, c, mine] = sendd[m, c, mine]

            def go(k, _):
                peer = (e + k) % PEERS
                rcopy(
                    sendd.at[m, c, pl.ds(peer * CAP, CAP)], recvd.at[m, c, mine], ds_sem.at[m, c], dr_sem.at[m, c], (p, peer)
                ).start()
                return 0

            lax.fori_loop(1, PEERS, go, 0)

        def wait_d(m, c):
            return rcopy(
                sendd.at[m, c, pl.ds(0, SLOTS - CAP)],
                recvd.at[m, c, pl.ds(0, SLOTS - CAP)],
                ds_sem.at[m, c],
                dr_sem.at[m, c],
                (p, e),
            )

        def send_r(m, c):
            def go(k, _):
                peer = (e + k) % PEERS
                rcopy(
                    sendr.at[m, c, pl.ds(peer * CAP, CAP)],
                    rets[m][c].at[mine],
                    rsnd_sem.at[m, c],
                    rr_sem.at[m, c],
                    (down, peer),
                ).start()
                return 0

            lax.fori_loop(0, PEERS, go, 0)

        def wait_r(m, c):
            return rcopy(sendr.at[m, c], rets[m][c], rsnd_sem.at[m, c], rr_sem.at[m, c], (down, e))

        def send_out(m):
            return rcopy(outstd.at[m], out_hbm.at[m], os_sem.at[m], or_sem.at[m], (up, e))

        in_x.wait()
        in_o.wait()
        in_t.wait()

        def tables(k, _):
            peer = (e + k) % PEERS
            rcopy(wtab.at[peer], wrecv.at[e], ts_sem, tr_sem, (p, peer)).start()
            return 0

        lax.fori_loop(1, PEERS, tables, 0)
        wrecv[e] = wtab[e]
        tabs = rcopy(wtab.at[pl.ds(0, PEERS - 1)], wrecv.at[pl.ds(0, PEERS - 1)], ts_sem, tr_sem, (p, e))

        for m in range(MB):
            xrow[pl.ds(m * T, T)] = xv[m].reshape(T, SUB, 128)
            send_x(m)

            @pl.when(top)
            def _():
                orow[pl.ds(m * T, T)] = ov[m].reshape(T, SUB, 128)
                for c in range(NC):
                    for k in range(SLOTS):
                        sendd[m, c, k] = orow[m * T + tok_ref[m * SLOTS + k], pl.ds(c * CS, CS), :]
                    send_d(m, c)

        gain = gain_ref.at[pl.ds(s, 1), :]
        QD = 512

        for c in lw:
            c.wait()
        for c in rw:
            c.wait_recv()
        tabs.wait_recv()

        def factors(m, _):
            wait_x(m).wait_recv()
            xstd[m] = recvx[m].reshape(SLOTS, D)
            for j in range(CAP):
                wrow[pl.ds(j, PEERS, stride=CAP), :] = wrecv[:, m * CAP + j, :]
            w = wrow[:, :1]

            def sq(i, acc):
                col = pl.ds(pl.multiple_of(i * QD, QD), QD)
                v = xstd[m, :, col].astype(F32)
                return acc + jnp.sum(v * v, axis=-1, keepdims=True)

            total = lax.fori_loop(0, D // QD, sq, jnp.zeros((SLOTS, 1), F32))
            r = lax.rsqrt(total * (1.0 / D) + EPS)
            rs[m] = jnp.broadcast_to(r, (SLOTS, 128))

            def norm(i, _):
                col = pl.ds(pl.multiple_of(i * QD, QD), QD)
                xn[:, col] = (xstd[m, :, col].astype(F32) * r * gain[:, col]).astype(BF)
                return 0

            lax.fori_loop(0, D // QD, norm, 0)
            gate = jnp.dot(xn[...], wg[...], preferred_element_type=F32)
            upv = jnp.dot(xn[...], wu[...], preferred_element_type=F32)
            q = jax.nn.sigmoid(gate)
            a = upv * q * (1.0 + gate * (1.0 - q))
            b = gate * q
            fa[m] = w * a
            fb[m] = w * b
            fc[m] = w * (a * gate + b * upv) * (1.0 / D)
            return 0

        lax.fori_loop(0, jnp.where(top, 1, MB), factors, 0)

        def home(m):
            for c in range(NC):
                wait_r(m, c).wait_recv()
                for k in range(SLOTS):
                    sendd[m, c, k] = rets[m][c][cidx_ref[m * SLOTS + k]]
                send_d(m, c)

        def output(m):
            for c in range(NC):
                for t in range(T):
                    fin[t, pl.ds(c * CS, CS), :] = rets[m][c][slotup_ref[m * T + t]]
            outstd[m] = fin[...].reshape(T, D)
            send_out(m).start()

        def chain(m, _):
            for i in range(MB):

                @pl.when(jnp.logical_and(m == i, jnp.logical_not(top)))
                def _():
                    home(i)

            lax.fori_loop(m + 1, jnp.where(jnp.logical_and(top, m < MB - 1), m + 2, m + 1), factors, 0)
            da = jnp.zeros((SLOTS, FF), F32)
            for c in range(NC):
                wait_d(m, c).wait_recv()
                dys[:, c * CD:(c + 1) * CD] = recvd[m, c].reshape(SLOTS, CD)
                da = da + dot_t(dys[:, c * CD:(c + 1) * CD], wd[:, c * CD:(c + 1) * CD])
            dg = (da * fa[m]).astype(BF)
            du = (da * fb[m]).astype(BF)
            r = rs[m][:, :1]
            mean = jnp.sum(da * fc[m], axis=-1, keepdims=True) * (r * r)
            for c in range(NC):
                for i in range(CD // QD):
                    col = pl.ds(c * CD + i * QD, QD)
                    con = dot_t(dg, wg[col, :]) + dot_t(du, wu[col, :])
                    res = dys[:, col].astype(F32) + (con * gain[:, col]) * r - xstd[m, :, col].astype(F32) * mean
                    ostd[:, pl.ds(i * QD, QD)] = res.astype(BF)
                sendr[m, c] = ostd[...].reshape(SLOTS, CS, 128)
                for i in range(MB):

                    @pl.when(m == i)
                    def _():
                        send_r(i, c)

            for i in range(MB):

                @pl.when(jnp.logical_and(m == i, jnp.logical_not(top)))
                def _():
                    output(i)

            return 0

        lax.fori_loop(0, MB, chain, 0)

        @pl.when(top)
        def _():
            for m in range(MB):
                for c in range(NC):
                    wait_r(m, c).wait_recv()
                output(m)

        for c in rw:
            c.wait_send()
        tabs.wait_send()
        for m in range(MB):
            wait_x(m).wait_send()
            for c in range(NC):
                wait_d(m, c).wait_send()
                wait_r(m, c).wait_send()
            send_out(m).wait()

    ret_t = pltpu.VMEM((SLOTS, CS, 128), BF)
    dma = pltpu.SemaphoreType.DMA
    scratch = [
        pltpu.VMEM((MB, T, D), BF),
        pltpu.VMEM((MB, T, D), BF),
        pltpu.VMEM((MB * T, SUB, 128), BF),
        pltpu.VMEM((MB * T, SUB, 128), BF),
        pltpu.VMEM((MB, SLOTS, SUB, 128), BF),
        pltpu.VMEM((MB, SLOTS, SUB, 128), BF),
        pltpu.VMEM((MB, NC, SLOTS, CS, 128), BF),
        pltpu.VMEM((MB, NC, SLOTS, CS, 128), BF),
        pltpu.VMEM((MB, NC, SLOTS, CS, 128), BF),
        pltpu.VMEM((MB, SLOTS, D), BF),
        pltpu.VMEM((SLOTS, D), BF),
        pltpu.VMEM((SLOTS, D), BF),
        pltpu.VMEM((SLOTS, CD), BF),
        pltpu.VMEM((MB, SLOTS, FF), F32),
        pltpu.VMEM((MB, SLOTS, FF), F32),
        pltpu.VMEM((MB, SLOTS, FF), F32),
        pltpu.VMEM((MB, SLOTS, 128), F32),
        pltpu.VMEM((PEERS, 16, 128), F32),
        pltpu.VMEM((PEERS, 16, 128), F32),
        pltpu.VMEM((SLOTS, 128), F32),
        pltpu.VMEM((D, FF), BF),
        pltpu.VMEM((D, FF), BF),
        pltpu.VMEM((FF, D), BF),
        pltpu.VMEM((T, SUB, 128), BF),
        pltpu.VMEM((MB, T, D), BF),
        *([ret_t] * (MB * NC)),
        dma((3,)),
        dma((3,)),
        dma((3,)),
        dma((3,)),
        dma,
        dma,
        dma((MB,)),
        dma((MB,)),
        dma((MB, NC)),
        dma((MB, NC)),
        dma((MB, NC)),
        dma((MB, NC)),
        dma((MB,)),
        dma((MB,)),
    ]
    return kernel, scratch


def on_device(section_inputs, out_grad, norm_gain, route_ids, route_weight, w_gate, w_up, w_down):
    lanes = lax.axis_size("pipe")
    peers = lax.axis_size("expert")
    micro, tok_rows, width = section_inputs.shape[1:]
    hidden = w_gate.shape[3]
    slots = peers * CAP
    ids = route_ids[0, :, :, 0]
    weights = route_weight[0, :, :, 0]
    onehot = (ids[:, :, None] == jnp.arange(peers, dtype=jnp.int32)).astype(jnp.int32)
    rank = jnp.cumsum(onehot, axis=1) - onehot
    slot = ids * CAP + jnp.sum(rank * onehot, axis=-1)
    slot_up = lax.ppermute(slot, "pipe", [((i + 2) % lanes, i) for i in range(lanes)])
    picked = slot[:, :, None] == jnp.arange(slots, dtype=jnp.int32)
    tok = jnp.sum(jnp.where(picked, jnp.arange(tok_rows, dtype=jnp.int32)[None, :, None], 0), axis=1)
    cidx = jnp.sum(jnp.where(picked, slot_up[:, :, None], 0), axis=1)
    wslot = jnp.sum(jnp.where(picked, weights[:, :, None], 0.0), axis=1)
    wtab = wslot.reshape(micro, peers, CAP).transpose(1, 0, 2).reshape(peers, micro * CAP)
    wtab = jnp.pad(wtab, ((0, 0), (0, 16 - micro * CAP)))
    wtab = jnp.broadcast_to(wtab[:, :, None], (peers, 16, 128))

    kernel, scratch = make_kernel(micro, tok_rows, width, hidden, lanes, peers)
    smem = pl.BlockSpec(memory_space=pltpu.SMEM)
    hbm = pl.BlockSpec(memory_space=pl.ANY)
    vmem = pl.BlockSpec(memory_space=pltpu.VMEM)
    out = pl.pallas_call(
        kernel,
        out_shape=jax.ShapeDtypeStruct((micro, tok_rows, width), BF),
        in_specs=[smem, smem, smem, hbm, hbm, hbm, vmem, hbm, hbm, hbm],
        out_specs=hbm,
        scratch_shapes=scratch,
        compiler_params=pltpu.CompilerParams(
            collective_id=0, has_side_effects=True, vmem_limit_bytes=58 * 1024 * 1024
        ),
        name="chain",
    )(
        tok.reshape(-1),
        cidx.reshape(-1),
        slot_up.reshape(-1),
        section_inputs[0],
        out_grad[0],
        wtab,
        norm_gain,
        w_gate[0, 0],
        w_up[0, 0],
        w_down[0, 0],
    )
    return out[None]


def solution(mesh):
    in_specs = (
        P("pipe", None, "expert", None),
        P("pipe", None, "expert", None),
        P(),
        P("pipe", None, "expert", None),
        P("pipe", None, "expert", None),
        P("pipe", "expert", None, None),
        P("pipe", "expert", None, None),
        P("pipe", "expert", None, None),
    )
    return jax.shard_map(
        on_device, mesh=mesh, in_specs=in_specs, out_specs=P("pipe", None, "expert", None), check_vma=False
    )
```

```python
import jax
import jax.numpy as jnp
from jax import lax
from jax.experimental import pallas as pl
from jax.experimental.pallas import tpu as pltpu
from jax.sharding import PartitionSpec as P

EPS = 1e-06
MESH = pl.DeviceIdType.MESH
BF = jnp.bfloat16
F32 = jnp.float32
CAP = 3
NC = 2


def dot_t(a, b):
    return lax.dot_general(a, b, (((1,), (1,)), ((), ())), preferred_element_type=F32)


def make_kernel(MB, T, D, FH, LANES, PEERS):
    SEC = LANES // 2
    SLOTS = PEERS * CAP
    SUB = D // 128
    CS = SUB // NC
    CD = D // NC
    FF = 2 * FH

    def kernel(tok_ref, cidx0_ref, cidx1_ref, slot_ref, slotup_ref, x_hbm, og_hbm, wtab_hbm, gain_ref, wg_hbm, wu_hbm, wd_hbm,
               out_hbm,
               xv, ov, xrow, orow, sendx, recvx, sendd0, sendd1, sendt1, recvd, sendr, xstd, xn, dys, ostd, fa, fb, fc, rs,
               wtab, wrecv, wrow, wg, wu, wd, wgt, wut, fin, outup, outown,
               ra0, ra1, ra2, ra3, rb0, rb1, rb2, rb3, rc0, rc1, rc2, rc3,
               in_sem, wl_sem, wrs_sem, wrr_sem, ts_sem, tr_sem, xs_sem, xr_sem, d0s_sem, d1s_sem, dts_sem, d0r_sem, d1r_sem,
               s0_sem, s1_sem, ra_sem, rb_sem, rc_sem, os_sem, or_sem, ol_sem):
        ra = (ra0, ra1, ra2, ra3)
        rb = (rb0, rb1, rb2, rb3)
        rc = (rc0, rc1, rc2, rc3)
        p = lax.axis_index("pipe")
        e = lax.axis_index("expert")
        s = p // 2
        h = p % 2
        down = (p + LANES - 2) % LANES
        up = (p + 2) % LANES
        mate = p + 1 - 2 * h
        top = s == SEC - 1
        low = jnp.logical_not(top)
        bottom = s == 0
        above = jnp.logical_not(bottom)
        both = jnp.logical_and

        def local_in(src, dst, i):
            return pltpu.make_async_copy(src, dst, in_sem.at[i])

        in_x = local_in(x_hbm, xv, 0)
        in_o = local_in(og_hbm, ov, 1)
        in_t = local_in(wtab_hbm, wtab, 2)
        in_x.start()
        in_t.start()
        in_o.start()
        part = pl.ds(pl.multiple_of(h * FH, 128), FH)
        lw = (
            pltpu.make_async_copy(wg_hbm, wg.at[:, part], wl_sem.at[0]),
            pltpu.make_async_copy(wu_hbm, wu.at[:, part], wl_sem.at[1]),
            pltpu.make_async_copy(wd_hbm, wd.at[part, :], wl_sem.at[2]),
        )
        for c in lw:
            c.start()

        barrier = pltpu.get_barrier_semaphore()

        def sig_plane(k, _):
            pl.semaphore_signal(barrier, inc=1, device_id=(p, (e + k) % PEERS), device_id_type=MESH)
            return 0

        lax.fori_loop(1, PEERS, sig_plane, 0)

        def sig_z(k, _):
            peer = (e + k) % PEERS
            pl.semaphore_signal(barrier, inc=1, device_id=(down, peer), device_id_type=MESH)
            pl.semaphore_signal(barrier, inc=1, device_id=(up, peer), device_id_type=MESH)
            return 0

        lax.fori_loop(0, PEERS, sig_z, 0)
        pl.semaphore_signal(barrier, inc=1, device_id=(mate, e), device_id_type=MESH)
        pl.semaphore_wait(barrier, PEERS - 1 + 2 * PEERS + 1)

        def rcopy(src, dst, ssem, rsem, dev):
            return pltpu.make_async_remote_copy(
                src_ref=src, dst_ref=dst, send_sem=ssem, recv_sem=rsem, device_id=dev, device_id_type=MESH
            )

        rw = (
            rcopy(wg_hbm, wg.at[:, part], wrs_sem.at[0], wrr_sem.at[0], (mate, e)),
            rcopy(wu_hbm, wu.at[:, part], wrs_sem.at[1], wrr_sem.at[1], (mate, e)),
            rcopy(wd_hbm, wd.at[part, :], wrs_sem.at[2], wrr_sem.at[2], (mate, e)),
        )
        for c in rw:
            c.start()

        mine = pl.ds(e * CAP, CAP)
        MOST = pl.ds(0, SLOTS - CAP)

        def scatter(src, dst, ssem, rsem, pipe, first):
            def go(k, _):
                peer = (e + k) % PEERS
                rcopy(src.at[pl.ds(peer * CAP, CAP)], dst.at[mine], ssem, rsem, (pipe, peer)).start()
                return 0

            lax.fori_loop(first, PEERS, go, 0)

        def arrived(buf, sem, self_too):
            v = buf if self_too else buf.at[MOST]
            return rcopy(v, v, sem, sem, (p, e)).wait_recv()

        def sent(buf, sem, self_too):
            v = buf if self_too else buf.at[MOST]
            return rcopy(v, v, sem, sem, (p, e)).wait_send()

        in_x.wait()
        in_t.wait()

        def tables(k, _):
            peer = (e + k) % PEERS
            rcopy(wtab.at[peer], wrecv.at[e], ts_sem, tr_sem, (p, peer)).start()
            return 0

        lax.fori_loop(1, PEERS, tables, 0)
        wrecv[e] = wtab[e]
        tabs = rcopy(wtab.at[pl.ds(0, PEERS - 1)], wrecv.at[pl.ds(0, PEERS - 1)], ts_sem, tr_sem, (p, e))
        in_o.wait()

        for m in range(MB):
            xrow[pl.ds(m * T, T)] = xv[m].reshape(T, SUB, 128)
            for k in range(SLOTS):
                sendx[m, k] = xrow[m * T + tok_ref[m * SLOTS + k]]
            recvx[m, mine] = sendx[m, mine]
            scatter(sendx.at[m], recvx.at[m], xs_sem.at[m], xr_sem.at[m], p, 1)

            @pl.when(top)
            def _():
                orow[pl.ds(m * T, T)] = ov[m].reshape(T, SUB, 128)
                for k in range(SLOTS):
                    sendd0[m, k] = orow[m * T + tok_ref[m * SLOTS + k], pl.ds(0, CS), :]
                recvd[m, 0, mine] = sendd0[m, mine]
                scatter(sendd0.at[m], recvd.at[m, 0], d0s_sem.at[m], d0r_sem.at[m], p, 1)
                for k in range(SLOTS):
                    sendt1[m, k] = orow[m * T + tok_ref[m * SLOTS + k], pl.ds(CS, CS), :]
                recvd[m, 1, mine] = sendt1[m, mine]
                scatter(sendt1.at[m], recvd.at[m, 1], dts_sem.at[m], d1r_sem.at[m], p, 1)

        gain = gain_ref.at[pl.ds(s, 1), :]
        QD = 512
        QE = 1024

        for c in lw:
            c.wait()
        for c in rw:
            c.wait_recv()
        tabs.wait_recv()

        def factors(m, _):
            arrived(recvx.at[m], xr_sem.at[m], False)
            xstd[m] = recvx[m].reshape(SLOTS, D)
            for j in range(CAP):
                wrow[pl.ds(j, PEERS, stride=CAP), :] = wrecv[:, m * CAP + j, :]
            w = wrow[:, :1]

            def sq(i, acc):
                col = pl.ds(pl.multiple_of(i * QD, QD), QD)
                v = xstd[m, :, col].astype(F32)
                return acc + jnp.sum(v * v, axis=-1, keepdims=True)

            total = lax.fori_loop(0, D // QD, sq, jnp.zeros((SLOTS, 1), F32))
            r = lax.rsqrt(total * (1.0 / D) + EPS)
            rs[m] = jnp.broadcast_to(r, (SLOTS, 128))

            def norm(i, _):
                col = pl.ds(pl.multiple_of(i * QD, QD), QD)
                xn[:, col] = (xstd[m, :, col].astype(F32) * r * gain[:, col]).astype(BF)
                return 0

            lax.fori_loop(0, D // QD, norm, 0)
            gate = jnp.dot(xn[...], wg[...], preferred_element_type=F32)
            upv = jnp.dot(xn[...], wu[...], preferred_element_type=F32)
            q = jax.nn.sigmoid(gate)
            a = upv * q * (1.0 + gate * (1.0 - q))
            b = gate * q
            fa[m] = w * a
            fb[m] = w * b
            fc[m] = w * (a * gate + b * upv) * (1.0 / D)
            return 0

        lax.fori_loop(0, jnp.where(top, 1, MB), factors, 0)

        @pl.when(low)
        def _():
            def flip(i, _):
                blk = pl.ds(pl.multiple_of(i * QD, QD), QD)
                wgt[:, blk] = wg[blk, :].T
                wut[:, blk] = wu[blk, :].T
                return 0

            lax.fori_loop(0, D // QD, flip, 0)

            def flipd(i, _):
                blk = pl.ds(pl.multiple_of(i * QD, QD), QD)
                wg[blk, :] = wd[:, blk].T
                return 0

            lax.fori_loop(0, D // QD, flipd, 0)

        def home0(m):
            arrived(ra[m], ra_sem.at[m], True)
            for k in range(SLOTS):
                sendd0[m, k] = ra[m][cidx0_ref[m * SLOTS + k]]
            recvd[m, 0, mine] = sendd0[m, mine]
            scatter(sendd0.at[m], recvd.at[m, 0], d0s_sem.at[m], d0r_sem.at[m], p, 1)

        def home1(m):
            for k in range(SLOTS):
                sendd1[m, k] = rb[m][cidx1_ref[m * SLOTS + k]]
            scatter(sendd1.at[m], recvd.at[m, 1], d1s_sem.at[m], d1r_sem.at[m], down, 0)

        def send_up(m):
            return rcopy(outup.at[m], out_hbm.at[m, :, pl.ds(0, CD)], os_sem.at[m], or_sem.at[m], (up, e))

        def own_out(m, c):
            return pltpu.make_async_copy(outown.at[m, c], out_hbm.at[m, :, pl.ds(c * CD, CD)], ol_sem.at[m, c])

        def expert(m, flat):
            arrived(recvd.at[m, 0], d0r_sem.at[m], False)

            def partial(c):
                dys[:, c * CD:(c + 1) * CD] = recvd[m, c].reshape(SLOTS, CD)
                v = dys[:, c * CD:(c + 1) * CD]
                if flat:
                    return jnp.dot(v, wg[c * CD:(c + 1) * CD, :], preferred_element_type=F32)
                return dot_t(v, wd[:, c * CD:(c + 1) * CD])

            da = partial(0)
            arrived(recvd.at[m, 1], d1r_sem.at[m], flat)
            da = da + partial(1)
            dg = (da * fa[m]).astype(BF)
            du = (da * fb[m]).astype(BF)
            r = rs[m][:, :1]
            mean = jnp.sum(da * fc[m], axis=-1, keepdims=True) * (r * r)
            for c in (1, 0):
                for i in range(CD // QE):
                    col = pl.ds(c * CD + i * QE, QE)
                    if flat:
                        con = jnp.dot(dg, wgt[:, col], preferred_element_type=F32)
                        con = con + jnp.dot(du, wut[:, col], preferred_element_type=F32)
                    else:
                        con = dot_t(dg, wg[col, :]) + dot_t(du, wu[col, :])
                    res = dys[:, col].astype(F32) + (con * gain[:, col]) * r - xstd[m, :, col].astype(F32) * mean
                    ostd[:, pl.ds(i * QE, QE)] = res.astype(BF)
                sendr[m, c] = ostd[...].reshape(SLOTS, CS, 128)
                for i in range(MB):

                    @pl.when(m == i)
                    def _():
                        if c == 1:
                            rb[i][mine] = sendr[i, 1, mine]
                            scatter(sendr.at[i, 1], rb[i], s1_sem.at[i], rb_sem.at[i], p, 1)
                        else:
                            if flat:

                                @pl.when(above)
                                def _():
                                    scatter(sendr.at[i, 0], ra[i], s0_sem.at[i], ra_sem.at[i], down, 0)

                                @pl.when(bottom)
                                def _():
                                    rc[i][mine] = sendr[i, 0, mine]
                                    scatter(sendr.at[i, 0], rc[i], s0_sem.at[i], rc_sem.at[i], p, 1)

                            else:
                                scatter(sendr.at[i, 0], ra[i], s0_sem.at[i], ra_sem.at[i], down, 0)

        def output(m):
            @pl.when(low)
            def _():
                for t in range(T):
                    fin[t] = ra[m][slotup_ref[m * T + t]]
                outup[m] = fin[...].reshape(T, CD)
                send_up(m).start()

            for t in range(T):
                fin[t] = rb[m][slot_ref[m * T + t]]
            outown[m, 1] = fin[...].reshape(T, CD)
            own_out(m, 1).start()

        @pl.when(low)
        def _():
            home0(0)

        def chain(m, _):
            @pl.when(top)
            def _():
                expert(m, False)

            @pl.when(low)
            def _():
                expert(m, True)

            lax.fori_loop(m + 1, jnp.where(both(top, m < MB - 1), m + 2, m + 1), factors, 0)
            for i in range(MB):

                @pl.when(m == i)
                def _():
                    if i + 1 < MB:

                        @pl.when(low)
                        def _():
                            home0(i + 1)

                    arrived(rb[i], rb_sem.at[i], False)

                    @pl.when(above)
                    def _():
                        home1(i)

                    output(i)

            return 0

        lax.fori_loop(0, MB, chain, 0)

        @pl.when(bottom)
        def _():
            for m in range(MB):
                arrived(rc[m], rc_sem.at[m], False)
                for t in range(T):
                    fin[t] = rc[m][slot_ref[m * T + t]]
                outown[m, 0] = fin[...].reshape(T, CD)
                own_out(m, 0).start()

        for c in rw:
            c.wait_send()
        tabs.wait_send()
        for m in range(MB):
            sent(sendx.at[m], xs_sem.at[m], False)
            sent(sendd0.at[m], d0s_sem.at[m], False)
            sent(sendr.at[m, 1], s1_sem.at[m], False)
            own_out(m, 1).wait()

            @pl.when(top)
            def _():
                sent(sendt1.at[m], dts_sem.at[m], False)

            @pl.when(low)
            def _():
                send_up(m).wait_send()

            @pl.when(above)
            def _():
                sent(sendd1.at[m], d1s_sem.at[m], True)
                sent(sendr.at[m, 0], s0_sem.at[m], True)
                send_up(m).wait_recv()

            @pl.when(bottom)
            def _():
                sent(sendr.at[m, 0], s0_sem.at[m], False)
                own_out(m, 0).wait()

    half_t = pltpu.VMEM((SLOTS, CS, 128), BF)
    halves = pltpu.VMEM((MB, SLOTS, CS, 128), BF)
    dma = pltpu.SemaphoreType.DMA
    scratch = [
        pltpu.VMEM((MB, T, D), BF),
        pltpu.VMEM((MB, T, D), BF),
        pltpu.VMEM((MB * T, SUB, 128), BF),
        pltpu.VMEM((MB * T, SUB, 128), BF),
        pltpu.VMEM((MB, SLOTS, SUB, 128), BF),
        pltpu.VMEM((MB, SLOTS, SUB, 128), BF),
        halves,
        halves,
        halves,
        pltpu.VMEM((MB, NC, SLOTS, CS, 128), BF),
        pltpu.VMEM((MB, NC, SLOTS, CS, 128), BF),
        pltpu.VMEM((MB, SLOTS, D), BF),
        pltpu.VMEM((SLOTS, D), BF),
        pltpu.VMEM((SLOTS, D), BF),
        pltpu.VMEM((SLOTS, CD), BF),
        pltpu.VMEM((MB, SLOTS, FF), F32),
        pltpu.VMEM((MB, SLOTS, FF), F32),
        pltpu.VMEM((MB, SLOTS, FF), F32),
        pltpu.VMEM((MB, SLOTS, 128), F32),
        pltpu.VMEM((PEERS, 16, 128), F32),
        pltpu.VMEM((PEERS, 16, 128), F32),
        pltpu.VMEM((SLOTS, 128), F32),
        pltpu.VMEM((D, FF), BF),
        pltpu.VMEM((D, FF), BF),
        pltpu.VMEM((FF, D), BF),
        pltpu.VMEM((FF, D), BF),
        pltpu.VMEM((FF, D), BF),
        pltpu.VMEM((T, CS, 128), BF),
        pltpu.VMEM((MB, T, CD), BF),
        pltpu.VMEM((MB, NC, T, CD), BF),
        *([half_t] * (3 * MB)),
        dma((3,)),
        dma((3,)),
        dma((3,)),
        dma((3,)),
        dma,
        dma,
        *([dma((MB,))] * 14),
        dma((MB, NC)),
    ]
    return kernel, scratch


def on_device(section_inputs, out_grad, norm_gain, route_ids, route_weight, w_gate, w_up, w_down):
    lanes = lax.axis_size("pipe")
    peers = lax.axis_size("expert")
    micro, tok_rows, width = section_inputs.shape[1:]
    hidden = w_gate.shape[3]
    slots = peers * CAP
    ids = route_ids[0, :, :, 0]
    weights = route_weight[0, :, :, 0]
    onehot = (ids[:, :, None] == jnp.arange(peers, dtype=jnp.int32)).astype(jnp.int32)
    rank = jnp.cumsum(onehot, axis=1) - onehot
    slot = ids * CAP + jnp.sum(rank * onehot, axis=-1)
    slot_up = lax.ppermute(slot, "pipe", [((i + 2) % lanes, i) for i in range(lanes)])
    picked = slot[:, :, None] == jnp.arange(slots, dtype=jnp.int32)
    tok = jnp.sum(jnp.where(picked, jnp.arange(tok_rows, dtype=jnp.int32)[None, :, None], 0), axis=1)
    cidx = jnp.sum(jnp.where(picked, slot_up[:, :, None], 0), axis=1)
    cidx_down = lax.ppermute(cidx, "pipe", [(i, (i + 2) % lanes) for i in range(lanes)])
    wslot = jnp.sum(jnp.where(picked, weights[:, :, None], 0.0), axis=1)
    wtab = wslot.reshape(micro, peers, CAP).transpose(1, 0, 2).reshape(peers, micro * CAP)
    wtab = jnp.pad(wtab, ((0, 0), (0, 16 - micro * CAP)))
    wtab = jnp.broadcast_to(wtab[:, :, None], (peers, 16, 128))

    kernel, scratch = make_kernel(micro, tok_rows, width, hidden, lanes, peers)
    smem = pl.BlockSpec(memory_space=pltpu.SMEM)
    hbm = pl.BlockSpec(memory_space=pl.ANY)
    vmem = pl.BlockSpec(memory_space=pltpu.VMEM)
    out = pl.pallas_call(
        kernel,
        out_shape=jax.ShapeDtypeStruct((micro, tok_rows, width), BF),
        in_specs=[smem, smem, smem, smem, smem, hbm, hbm, hbm, vmem, hbm, hbm, hbm],
        out_specs=hbm,
        scratch_shapes=scratch,
        compiler_params=pltpu.CompilerParams(
            collective_id=0, has_side_effects=True, vmem_limit_bytes=58 * 1024 * 1024
        ),
        name="chain",
    )(
        tok.reshape(-1),
        cidx.reshape(-1),
        cidx_down.reshape(-1),
        slot.reshape(-1),
        slot_up.reshape(-1),
        section_inputs[0],
        out_grad[0],
        wtab,
        norm_gain,
        w_gate[0, 0],
        w_up[0, 0],
        w_down[0, 0],
    )
    return out[None]


def solution(mesh):
    in_specs = (
        P("pipe", None, "expert", None),
        P("pipe", None, "expert", None),
        P(),
        P("pipe", None, "expert", None),
        P("pipe", None, "expert", None),
        P("pipe", "expert", None, None),
        P("pipe", "expert", None, None),
        P("pipe", "expert", None, None),
    )
    return jax.shard_map(
        on_device, mesh=mesh, in_specs=in_specs, out_specs=P("pipe", None, "expert", None), check_vma=False
    )
```
